128 devices in a mesh: img: 8 (over x, core), pos: 16 (over z, y).
Axes of the slice: x: 4, y: 4, z: 4, core: 2. Of those that a mesh axis runs over, the one named last changes fastest.
Arguments:
- features: bfloat16 [16384, 32, 1536], P(('img', 'pos')), may hold values from -6 to 6
- channel_index: int32 [550], replicated, may hold values from 0 to 1535, as said below
- image_counts: int32 [128], P(('img', 'pos')), may hold values from 32 to 128, as said below
Outputs:
- centres: float32 [32, 550], P('pos')
- covars: float32 [32, 550, 550], P('pos')
The draws below stay inside these ranges and needn't reach their ends.
Inputs may be any that keep to these rules, and one draw needn't show every extreme that they name: `channel_index`: distinct channel numbers. `image_counts`: some device uses all 128 slots and some only a quarter.
All inputs are finite; a program needn't handle non-finite values.
Results may differ from the reference program's by a relative error of at most 0.0003.
Values may be sent and summed in bfloat16 or wider, within the bound.
A program may use at most 128 MiB of HBM per device.

```python
import jax
import jax.numpy as jnp
from jax import lax

C_IN = 1536
K = 550
IMG_DEV = 128
POS = 32
IMAGES = 16384
DEVICES = 128


def draw_channel_index(key, part):
    return jax.random.permutation(jax.random.fold_in(key, 11), C_IN)[:K].astype(jnp.int32)


def draw_image_counts(key, part):
    key_vals = jax.random.fold_in(key, 21)
    key_perm = jax.random.fold_in(key, 22)
    values = jax.random.randint(key_vals, (DEVICES,), IMG_DEV // 4, IMG_DEV + 1).astype(jnp.int32)
    order = jax.random.permutation(key_perm, DEVICES)
    values = values.at[order[0]].set(IMG_DEV)
    values = values.at[order[1]].set(IMG_DEV // 4)
    return values


def shard_levels(key, extent, split, smallest, largest):
    loudness = 1.0
    for dim, shards_of in split:
        draws = jax.random.uniform(jax.random.fold_in(jax.random.fold_in(key, 6), dim), (shards_of,), jnp.float32, smallest / len(split), largest / len(split))
        loudness = loudness * jnp.repeat(jnp.exp(draws), extent[dim] // shards_of).reshape((-1,) + (1,) * (len(extent) - 1 - dim))
    return loudness


def bell_draw(key, extent, width, reach, pieces=(), kind=jnp.bfloat16):
    result = width * jax.random.normal(key, extent, jnp.float32)
    if pieces:
        result = result * shard_levels(key, extent, pieces, -0.22, 0.18)
    return jnp.clip(result, -reach, reach).astype(kind)


def setup_inputs(seed: int = 0) -> dict:
    seeds = jax.random.split(jax.random.key(seed), 4)
    return {
        "features": bell_draw(seeds[0], (IMAGES, POS, C_IN), 1.0, 6.0, ((0, 128),)),
        "channel_index": draw_channel_index(jax.random.fold_in(seeds[3], 71), 0),
        "image_counts": draw_image_counts(jax.random.fold_in(seeds[3], 71), 0),
    }


REG = 0.01


def reference(features, channel_index, image_counts):
    images = features.shape[0]
    slot_index = jnp.arange(images, dtype=jnp.int32)
    usable = (slot_index % IMG_DEV) < image_counts[slot_index // IMG_DEV]
    weight_row = usable.astype(jnp.float32)
    total_count = jnp.sum(image_counts.astype(jnp.float32))
    identity_mat = jnp.eye(K, dtype=jnp.float32)

    def one_position(position):
        at_position = lax.dynamic_index_in_dim(features, position, 1, keepdims=False)
        chosen = jnp.take(at_position, channel_index, axis=1).astype(jnp.float32) * weight_row[:, None]
        sq_sum = jnp.dot(chosen.T, chosen, precision=lax.Precision.HIGHEST)
        lin_sum = jnp.sum(chosen, axis=0)
        centre = lin_sum / total_count
        scatter_mat = sq_sum - total_count * jnp.outer(centre, centre)
        return centre, scatter_mat / (total_count - 1.0) + REG * identity_mat

    centres, covars = lax.map(one_position, jnp.arange(POS, dtype=jnp.int32))
    return centres, covars
```

```python
import functools

import jax
import jax.numpy as jnp
from jax import lax
from jax.experimental import pallas as pl
from jax.experimental.pallas import tpu as pltpu
from jax.sharding import PartitionSpec as P

REG = 0.01
MESH = pl.DeviceIdType.MESH
RING = 4
LANE = 128
F32 = jnp.float32
BF16 = jnp.bfloat16


def sizes(width):
    rows = -(-(width + 1) // 16) * 16
    full = rows // LANE
    strip = rows - full * LANE
    packed = full * (full + 1) // 2 * LANE + strip * (full + 1)
    return rows, full, strip, -(-packed // 32) * 32


def block_row(i, full, strip):
    return i * (i + 1) // 2 * LANE, (LANE if i < full else strip)


def gather_kernel(
    width, feat, chan, count, out,
    slab, onehot, picked, send, recv, part, rs_recv, ar_recv, tot,
    load_sem, send_sem, recv_sem, rs_send, rs_sem, ar_send, ar_sem, ag_send, ag_sem, fw_send, fw_sem, out_sem,
):
    rows, full, strip, packed = sizes(width)
    piece = packed // RING
    images, owned = feat.shape[0], feat.shape[1] // RING
    c_in, cols = onehot.shape
    img, pos = lax.axis_index("img"), lax.axis_index("pos")
    x, c = img // 2, img % 2
    z, y = pos // RING, pos % RING
    ring_b = (1 - c) * y + c * z

    barrier = pltpu.get_barrier_semaphore()

    def greet(i, p):
        pl.semaphore_signal(barrier, inc=1, device_id={"img": i, "pos": p}, device_id_type=MESH)

    for d in range(1, RING):
        for k in range(2):
            greet(2 * x + k, (z + d) % RING * RING + y)
            greet(2 * x + k, z * RING + (y + d) % RING)
        greet((x + d) % RING * 2 + c, pos)
    greet(2 * x + 1 - c, pos)

    def load(t):
        zp = (z + 1 + t) % RING
        return pltpu.make_async_copy(
            feat.at[:, pl.ds(zp * owned, owned), :], slab.at[t], load_sem.at[t]
        )

    for t in range(RING):
        load(t).start()

    tail = width // LANE * LANE
    onehot[:, tail:] = jnp.zeros((c_in, cols - tail), BF16)
    step = 256

    def build(i, carry):
        at = pl.ds(pl.multiple_of(i * step, step), step)
        which = lax.broadcasted_iota(jnp.int32, (step, width), 0) + i * step
        onehot[at, :width] = jnp.where(which == chan[...], 1.0, 0.0).astype(BF16)
        return carry

    lax.fori_loop(0, c_in // step, build, 0)
    last = full * (full + 1) // 2 * LANE + strip * full
    for b in range(RING):
        part[b, last:, :] = jnp.zeros((packed - last, LANE), F32)

    usable = lax.broadcasted_iota(jnp.int32, (LANE, images), 1) < count[0]
    is_one = lax.broadcasted_iota(jnp.int32, (LANE, images), 0) == width % LANE
    pl.semaphore_wait(barrier, 5 * (RING - 1) + 1)

    def pick(t, carry):
        zp = (z + 1 + t) % RING
        load(t).wait()
        group = 32

        def multiply(g, carry):
            at = pl.ds(pl.multiple_of(g * group, group), group)
            chunk = slab[t, at].reshape(group * owned, c_in)
            to = pl.ds(pl.multiple_of(g * group * owned, group * owned), group * owned)
            found = jnp.dot(chunk, onehot[...], preferred_element_type=F32)
            for l in range(cols // LANE):
                picked[l, to, :] = found[:, l * LANE:(l + 1) * LANE]
            return carry

        lax.fori_loop(0, images // group, multiply, 0)
        for j in range(owned):
            yp, k = j // 2, j % 2
            for l in range(cols // LANE):
                height = min(LANE, rows - l * LANE)
                block = picked[l, pl.ds(j, images, stride=owned), :].T[:height]
                if l == width // LANE:
                    block = jnp.where(is_one[:height], 1.0, block)
                block = jnp.where(usable[:height], block, 0.0)
                send[zp, j, l * LANE:l * LANE + height, :] = block.astype(BF16)
            if k == 0:
                to_pos, b, a = zp * RING + y, yp, z
                mine = (c == 0) & (zp == z)
            else:
                to_pos, b, a = z * RING + yp, zp, y
                mine = (c == 1) & (yp == y)
            dst = recv.at[b, :, pl.ds(pl.multiple_of(a * 2 * LANE + c * LANE, LANE), LANE)]

            @pl.when(mine)
            def _():
                pltpu.make_async_copy(send.at[zp, j], dst, recv_sem.at[b, a * 2 + c]).start()

            @pl.when(jnp.logical_not(mine))
            def _():
                pltpu.make_async_remote_copy(
                    src_ref=send.at[zp, j], dst_ref=dst,
                    send_sem=send_sem.at[zp, j], recv_sem=recv_sem.at[b, a * 2 + c],
                    device_id={"img": 2 * x + k, "pos": to_pos}, device_id_type=MESH,
                ).start()

        return carry

    lax.fori_loop(0, RING, pick, 0)

    def rs_copy(b):
        to_pos = (1 - c) * (z * RING + b) + c * (b * RING + y)
        return pltpu.make_async_remote_copy(
            src_ref=part.at[b], dst_ref=rs_recv.at[ring_b],
            send_sem=rs_send.at[b], recv_sem=rs_sem.at[ring_b],
            device_id={"img": img, "pos": to_pos}, device_id_type=MESH,
        )

    def gram(t, carry):
        b = (ring_b + 1 + t) % RING
        for s in range(2 * RING):
            pltpu.make_async_copy(
                send.at[0, 0], recv.at[b, :, s * LANE:(s + 1) * LANE], recv_sem.at[b, s]
            ).wait()
        for i in range(full + (strip > 0)):
            first, height = block_row(i, full, strip)
            wide = min((i + 1) * LANE, rows)
            prod = lax.dot_general(
                recv[b, i * LANE:i * LANE + height, :], recv[b, :wide, :],
                (((1,), (1,)), ((), ())), preferred_element_type=F32,
            )
            for j in range(i + 1):
                w = min(LANE, wide - j * LANE)
                part[b, first + j * height:first + (j + 1) * height, :w] = prod[:, j * LANE:j * LANE + w]

        @pl.when(t < RING - 1)
        def _():
            rs_copy(b).start()

        return carry

    lax.fori_loop(0, RING, gram, 0)

    def rs_wait(d, carry):
        b = (ring_b + d) % RING
        pltpu.make_async_copy(part.at[0], rs_recv.at[b], rs_sem.at[b]).wait()
        part[ring_b] = part[ring_b] + rs_recv[b]
        return carry

    lax.fori_loop(1, RING, rs_wait, 0)

    def rows_of(q):
        return pl.ds(pl.multiple_of(q * piece, 8), piece)

    def ar_copy(d):
        q = (x + d) % RING
        return pltpu.make_async_remote_copy(
            src_ref=part.at[ring_b, rows_of(q)], dst_ref=ar_recv.at[x],
            send_sem=ar_send.at[q], recv_sem=ar_sem.at[x],
            device_id={"img": 2 * q + c, "pos": pos}, device_id_type=MESH,
        )

    def ag_copy(d):
        q = (x + d) % RING
        return pltpu.make_async_remote_copy(
            src_ref=tot.at[c, rows_of(x)], dst_ref=tot.at[c, rows_of(x)],
            send_sem=ag_send.at[q], recv_sem=ag_sem.at[x],
            device_id={"img": 2 * q + c, "pos": pos}, device_id_type=MESH,
        )

    def fw_copy(q):
        return pltpu.make_async_remote_copy(
            src_ref=tot.at[c, rows_of(q)], dst_ref=tot.at[c, rows_of(q)],
            send_sem=fw_send.at[q], recv_sem=fw_sem.at[q],
            device_id={"img": 2 * x + 1 - c, "pos": pos}, device_id_type=MESH,
        )

    for d in (2, 1, 3):
        ar_copy(d).start()
    total = part[ring_b, rows_of(x)]
    for d in (1, 3, 2):
        q = (x + d) % RING
        pltpu.make_async_copy(part.at[0, rows_of(0)], ar_recv.at[q], ar_sem.at[q]).wait()
        total = total + ar_recv[q]
    tot[c, rows_of(x)] = total
    for d in (2, 1, 3):
        ag_copy(d).start()
    fw_copy(x).start()
    for d in (1, 3, 2):
        q = (x + d) % RING
        pltpu.make_async_copy(part.at[0, rows_of(0)], tot.at[c, rows_of(q)], ag_sem.at[q]).wait()
        fw_copy(q).start()
    for q in range(RING):
        pltpu.make_async_copy(part.at[0, rows_of(0)], tot.at[1 - c, rows_of(q)], fw_sem.at[q]).wait()
    write = pltpu.make_async_copy(tot, out, out_sem)
    write.start()

    def sent(t, carry):
        zp = (z + 1 + t) % RING
        for j in range(owned):
            yp, k = j // 2, j % 2
            mine = (c == k) & ((zp == z) if k == 0 else (yp == y))

            @pl.when(jnp.logical_not(mine))
            def _():
                pltpu.make_async_copy(send.at[zp, j], send.at[zp, j], send_sem.at[zp, j]).wait()

        return carry

    lax.fori_loop(0, RING, sent, 0)
    for d in range(1, RING):
        rs_copy((ring_b + d) % RING).wait_send()
        ar_copy(d).wait_send()
        ag_copy(d).wait_send()
    for q in range(RING):
        fw_copy(q).wait_send()
    write.wait()


def finish_kernel(width, tot, centres, covars):
    rows, full, strip, packed = sizes(width)

    def block(p, i, j):
        first, height = block_row(i, full, strip)
        return tot[p, first + j * height:first + (j + 1) * height, :]

    mark = width - full * LANE
    for p in range(tot.shape[0]):
        lin = jnp.concatenate([block(p, full, j)[mark:mark + 1] for j in range(full + 1)], axis=1)
        n = block(p, full, full)[mark:mark + 1, mark:mark + 1]
        centre = lin / n
        centres[p:p + 1, :] = centre[:, :width]
        for i in range(full + 1):
            height = block_row(i, full, strip)[1]
            parts = [block(p, i, j) for j in range(i + 1)]
            for j in range(i + 1, full + 1):
                flip = block(p, j, i).T
                if flip.shape[1] < LANE:
                    flip = jnp.concatenate([flip, jnp.zeros((height, LANE - flip.shape[1]), F32)], axis=1)
                parts.append(flip)
            sums = jnp.concatenate(parts, axis=1)
            own = sums[:, width:width + 1] / n
            spread = (sums - n * (own * centre)) / (n - 1.0)
            row = lax.broadcasted_iota(jnp.int32, sums.shape, 0) + i * LANE
            col = lax.broadcasted_iota(jnp.int32, sums.shape, 1)
            spread = spread + jnp.where(row == col, REG, 0.0)
            keep = min(height, width - i * LANE)
            covars[p, i * LANE:i * LANE + keep, :] = spread[:keep, :width]


def body(features, channel_index, image_counts):
    images, positions, c_in = features.shape
    width = channel_index.shape[0]
    rows, full, strip, packed = sizes(width)
    cols = -(-rows // LANE) * LANE
    owned = positions // RING
    dma = pltpu.SemaphoreType.DMA
    tot = pl.pallas_call(
        functools.partial(gather_kernel, width),
        out_shape=jax.ShapeDtypeStruct((2, packed, LANE), F32),
        in_specs=[
            pl.BlockSpec(memory_space=pl.ANY),
            pl.BlockSpec(memory_space=pltpu.VMEM),
            pl.BlockSpec(memory_space=pltpu.SMEM),
        ],
        out_specs=pl.BlockSpec(memory_space=pl.ANY),
        scratch_shapes=[
            pltpu.VMEM((RING, images, owned, c_in), BF16),
            pltpu.VMEM((c_in, cols), BF16),
            pltpu.VMEM((cols // LANE, images * owned, LANE), F32),
            pltpu.VMEM((RING, owned, rows, images), BF16),
            pltpu.VMEM((RING, rows, 2 * RING * LANE), BF16),
            pltpu.VMEM((RING, packed, LANE), F32),
            pltpu.VMEM((RING, packed, LANE), F32),
            pltpu.VMEM((RING, packed // RING, LANE), F32),
            pltpu.VMEM((2, packed, LANE), F32),
            dma((RING,)),
            dma((RING, owned)),
            dma((RING, 2 * RING)),
            dma((RING,)), dma((RING,)),
            dma((RING,)), dma((RING,)),
            dma((RING,)), dma((RING,)),
            dma((RING,)), dma((RING,)),
            dma,
        ],
        compiler_params=pltpu.CompilerParams(
            collective_id=0, has_side_effects=True, vmem_limit_bytes=56 * 2**20
        ),
        name="pick_and_sum",
    )(features, channel_index.reshape(1, width), image_counts)
    return pl.pallas_call(
        functools.partial(finish_kernel, width),
        out_shape=(
            jax.ShapeDtypeStruct((2, width), F32),
            jax.ShapeDtypeStruct((2, width, width), F32),
        ),
        in_specs=[pl.BlockSpec(memory_space=pltpu.VMEM)],
        out_specs=(pl.BlockSpec(memory_space=pltpu.VMEM), pl.BlockSpec(memory_space=pltpu.VMEM)),
        compiler_params=pltpu.CompilerParams(vmem_limit_bytes=40 * 2**20),
        name="finish",
    )(tot)


def solution(mesh):
    placed = (P(("img", "pos"), None, None), P(), P(("img", "pos")))
    return jax.shard_map(
        body,
        mesh=mesh,
        in_specs=placed,
        out_specs=(P("pos", None), P("pos", None, None)),
        check_vma=False,
    )
```

```python
import functools

import jax
import jax.numpy as jnp
from jax import lax
from jax.experimental import pallas as pl
from jax.experimental.pallas import tpu as pltpu
from jax.sharding import PartitionSpec as P

REG = 0.01
MESH = pl.DeviceIdType.MESH
RING = 4
LANE = 128
F32 = jnp.float32
BF16 = jnp.bfloat16


def sizes(width):
    rows = -(-(width + 1) // 16) * 16
    full = (width + 1) // LANE // 2 * 2
    strip = -(-(width + 1 - full * LANE) // 8) * 8
    packed = full * full // 2 * LANE + strip * (full + 1) + full // 2
    return rows, full, strip, -(-packed // 32) * 32


def place(i, j, full, strip):
    if i == full:
        return full * full // 2 * LANE + j * strip
    if i == j:
        return (full * (full - 1) // 2 + i // 2) * LANE
    return (i * (i - 1) // 2 + j) * LANE


def gather_kernel(
    width, feat, chan, count, tot,
    slab, onehot, picked, send, recv, part, x_recv, owned_sum, b_recv,
    load_sem, send_sem, recv_sem, x_send, x_sem, b_send, b_sem, ag_send, ag_sem, fw_send, fw_sem,
):
    rows, full, strip, packed = sizes(width)
    piece = packed // RING
    images, owned = feat.shape[0], feat.shape[1] // RING
    c_in, cols = onehot.shape
    img, pos = lax.axis_index("img"), lax.axis_index("pos")
    x, c = img // 2, img % 2
    z, y = pos // RING, pos % RING
    ring_b = (1 - c) * y + c * z

    barrier = pltpu.get_barrier_semaphore()

    def greet(i, p):
        pl.semaphore_signal(barrier, inc=1, device_id={"img": i, "pos": p}, device_id_type=MESH)

    for d in range(1, RING):
        for k in range(2):
            greet(2 * x + k, (z + d) % RING * RING + y)
            greet(2 * x + k, z * RING + (y + d) % RING)
        greet((x + d) % RING * 2 + c, pos)
    greet(2 * x + 1 - c, pos)

    def load(t):
        zp = (z + 1 + t) % RING
        return pltpu.make_async_copy(
            feat.at[:, pl.ds(zp * owned, owned), :], slab.at[t], load_sem.at[t]
        )

    for t in range(RING):
        load(t).start()

    tail = width // LANE * LANE
    onehot[:, tail:] = jnp.zeros((c_in, cols - tail), BF16)
    step = 256

    def build(i, carry):
        at = pl.ds(pl.multiple_of(i * step, step), step)
        which = lax.broadcasted_iota(jnp.int32, (step, width), 0) + i * step
        onehot[at, :width] = jnp.where(which == chan[...].reshape(1, width), 1.0, 0.0).astype(BF16)
        return carry

    lax.fori_loop(0, c_in // step, build, 0)
    last = place(full, full, full, strip)
    for b in range(RING):
        part[b, last:, :] = jnp.zeros((packed - last, LANE), F32)

    usable = lax.broadcasted_iota(jnp.int32, (LANE, images), 1) < count[0]
    is_one = lax.broadcasted_iota(jnp.int32, (LANE, images), 0) == width % LANE
    pl.semaphore_wait(barrier, 5 * (RING - 1) + 1)

    def exchange(zp, yp, k):
        to_pos = zp * RING + y if k == 0 else z * RING + yp
        b, a = (yp, z) if k == 0 else (zp, y)
        mine = (c == k) & (to_pos == pos)
        src = send.at[zp, 2 * yp + k]
        dst = recv.at[b, :, pl.ds(pl.multiple_of(a * 2 * LANE + c * LANE, LANE), LANE)]

        @pl.when(mine)
        def _():
            pltpu.make_async_copy(src, dst, recv_sem.at[b, a * 2 + c]).start()

        @pl.when(jnp.logical_not(mine))
        def _():
            pltpu.make_async_remote_copy(
                src_ref=src, dst_ref=dst,
                send_sem=send_sem.at[zp, 2 * yp + k], recv_sem=recv_sem.at[b, a * 2 + c],
                device_id={"img": 2 * x + k, "pos": to_pos}, device_id_type=MESH,
            ).start()

    def pick(t, carry):
        zp = (z + 1 + t) % RING
        load(t).wait()
        group = images

        def multiply(g, carry):
            at = pl.ds(pl.multiple_of(g * group, group), group)
            chunk = slab[t, at].reshape(group * owned, c_in)
            to = pl.ds(pl.multiple_of(g * group * owned, group * owned), group * owned)
            found = jnp.dot(chunk, onehot[...], preferred_element_type=F32)
            for l in range(cols // LANE):
                picked[l, to, :] = found[:, l * LANE:(l + 1) * LANE]
            return carry

        lax.fori_loop(0, images // group, multiply, 0)
        for j in range(owned):
            yp, k = j // 2, j % 2
            for l in range(cols // LANE):
                height = min(LANE, rows - l * LANE)
                block = picked[l, pl.ds(j, images, stride=owned), :].T[:height]
                if l == width // LANE:
                    block = jnp.where(is_one[:height], 1.0, block)
                block = jnp.where(usable[:height], block, 0.0)
                send[zp, j, l * LANE:l * LANE + height, :] = block.astype(BF16)
            if k == 0:
                @pl.when(((yp - y + RING) % RING == 1) | ((yp - y + RING) % RING == 2))
                def _():
                    exchange(zp, yp, 0)
            else:
                exchange(zp, yp, 1)

        return carry

    lax.fori_loop(0, RING, pick, 0)

    def rest(t, carry):
        exchange((z + 1 + t % RING) % RING, (y + 3 + t // RING) % RING, 0)
        return carry

    lax.fori_loop(0, 2 * RING, rest, 0)

    def rows_of(q):
        return pl.ds(pl.multiple_of(q * piece, 8), piece)

    def x_copy(b, d):
        q = (x + d) % RING
        return pltpu.make_async_remote_copy(
            src_ref=part.at[b, rows_of(q)], dst_ref=x_recv.at[b, x],
            send_sem=x_send.at[b, q], recv_sem=x_sem.at[b, x],
            device_id={"img": 2 * q + c, "pos": pos}, device_id_type=MESH,
        )

    def b_copy(b):
        to_pos = (1 - c) * (z * RING + b) + c * (b * RING + y)
        return pltpu.make_async_remote_copy(
            src_ref=owned_sum.at[b], dst_ref=b_recv.at[ring_b],
            send_sem=b_send.at[b], recv_sem=b_sem.at[ring_b],
            device_id={"img": img, "pos": to_pos}, device_id_type=MESH,
        )

    row = lax.broadcasted_iota(jnp.int32, (LANE, LANE), 0)
    col = lax.broadcasted_iota(jnp.int32, (LANE, LANE), 1)

    def gram(t):
        b = (ring_b + 1 + t) % RING
        for s in range(2 * RING):
            pltpu.make_async_copy(
                send.at[0, 0], recv.at[b, :, s * LANE:(s + 1) * LANE], recv_sem.at[b, s]
            ).wait()
        for i in range(full + 1):
            height, wide = (LANE, (i + 1) * LANE) if i < full else (strip, full * LANE + strip)
            prod = lax.dot_general(
                recv[b, i * LANE:i * LANE + height, :], recv[b, :wide, :],
                (((1,), (1,)), ((), ())), preferred_element_type=F32,
            )
            for j in range(i + 1):
                first = place(i, j, full, strip)
                w = min(LANE, wide - j * LANE)
                block = prod[:, j * LANE:j * LANE + w]
                if i == j and i % 2 == 1:
                    at = place(full, full, full, strip) + strip + i // 2
                    part[b, at:at + 1, :] = jnp.sum(jnp.where(row == col, block, 0.0), axis=0, keepdims=True)
                    block = jnp.where(row >= col, part[b, first:first + LANE, :], block)
                part[b, first:first + height, :w] = block
        for d in (2, 1, 3):
            x_copy(b, d).start()

    def settle(t):
        b = (ring_b + 1 + t) % RING
        total = part[b, rows_of(x)]
        for d in (1, 3, 2):
            q = (x + d) % RING
            pltpu.make_async_copy(owned_sum.at[0], x_recv.at[b, q], x_sem.at[b, q]).wait()
            total = total + x_recv[b, q]
        owned_sum[b] = total

    gram(0)

    def stage(t, carry):
        gram(t)
        settle(t - 1)
        b_copy((ring_b + t) % RING).start()
        return carry

    lax.fori_loop(1, RING, stage, 0)
    settle(RING - 1)

    def ag_copy(d):
        q = (x + d) % RING
        return pltpu.make_async_remote_copy(
            src_ref=tot.at[c, rows_of(x)], dst_ref=tot.at[c, rows_of(x)],
            send_sem=ag_send.at[q], recv_sem=ag_sem.at[x],
            device_id={"img": 2 * q + c, "pos": pos}, device_id_type=MESH,
        )

    def fw_copy(q):
        return pltpu.make_async_remote_copy(
            src_ref=tot.at[c, rows_of(q)], dst_ref=tot.at[c, rows_of(q)],
            send_sem=fw_send.at[q], recv_sem=fw_sem.at[q],
            device_id={"img": 2 * x + 1 - c, "pos": pos}, device_id_type=MESH,
        )

    total = owned_sum[ring_b]
    for d in (1, 2, 3):
        b = (ring_b + d) % RING
        pltpu.make_async_copy(owned_sum.at[0], b_recv.at[b], b_sem.at[b]).wait()
        total = total + b_recv[b]
    tot[c, rows_of(x)] = total
    for d in (2, 1, 3):
        ag_copy(d).start()
    fw_copy(x).start()
    for d in (1, 3, 2):
        q = (x + d) % RING
        pltpu.make_async_copy(owned_sum.at[0], tot.at[c, rows_of(q)], ag_sem.at[q]).wait()
        fw_copy(q).start()
    for q in range(RING):
        pltpu.make_async_copy(owned_sum.at[0], tot.at[1 - c, rows_of(q)], fw_sem.at[q]).wait()

    def sent(t, carry):
        zp = (z + 1 + t) % RING
        for j in range(owned):
            yp, k = j // 2, j % 2
            mine = (c == k) & ((zp == z) if k == 0 else (yp == y))

            @pl.when(jnp.logical_not(mine))
            def _():
                pltpu.make_async_copy(send.at[zp, j], send.at[zp, j], send_sem.at[zp, j]).wait()

        return carry

    lax.fori_loop(0, RING, sent, 0)
    for d in range(1, RING):
        b_copy((ring_b + d) % RING).wait_send()
        for b in range(RING):
            x_copy(b, d).wait_send()
        ag_copy(d).wait_send()
    for q in range(RING):
        fw_copy(q).wait_send()


def finish_kernel(width, tot, centres, covars):
    rows, full, strip, packed = sizes(width)
    row = lax.broadcasted_iota(jnp.int32, (LANE, LANE), 0)
    col = lax.broadcasted_iota(jnp.int32, (LANE, LANE), 1)
    diagonals = place(full, full, full, strip) + strip

    def block(p, i, j):
        first = place(i, j, full, strip)
        if i == full:
            return tot[p, first:first + strip, :]
        both = tot[p, first:first + LANE, :]
        if i > j:
            return both
        if i % 2 == 0:
            return jnp.where(row >= col, both, both.T)
        at = diagonals + i // 2
        return jnp.where(row == col, tot[p, at:at + 1, :], jnp.where(row < col, both, both.T))

    mark = width - full * LANE
    for p in range(tot.shape[0]):
        lin = jnp.concatenate([block(p, full, j)[mark:mark + 1] for j in range(full + 1)], axis=1)
        n = block(p, full, full)[mark:mark + 1, mark:mark + 1]
        centre = lin / n
        centres[p:p + 1, :] = centre[:, :width]
        for i in range(full + 1):
            height = LANE if i < full else strip
            parts = [block(p, i, j) for j in range(i + 1)]
            for j in range(i + 1, full + 1):
                flip = block(p, j, i).T
                if flip.shape[1] < LANE:
                    flip = jnp.concatenate([flip, jnp.zeros((height, LANE - flip.shape[1]), F32)], axis=1)
                parts.append(flip)
            sums = jnp.concatenate(parts, axis=1)
            own = sums[:, width:width + 1] / n
            spread = (sums - n * (own * centre)) / (n - 1.0)
            at = lax.broadcasted_iota(jnp.int32, sums.shape, 0) + i * LANE
            across = lax.broadcasted_iota(jnp.int32, sums.shape, 1)
            spread = spread + jnp.where(at == across, REG, 0.0)
            keep = min(height, width - i * LANE)
            covars[i * LANE:i * LANE + keep, p, :] = spread[:keep, :width]


def body(features, channel_index, image_counts):
    images, positions, c_in = features.shape
    width = channel_index.shape[0]
    rows, full, strip, packed = sizes(width)
    cols = -(-rows // LANE) * LANE
    owned = positions // RING
    dma = pltpu.SemaphoreType.DMA
    tot = pl.pallas_call(
        functools.partial(gather_kernel, width),
        out_shape=jax.ShapeDtypeStruct((2, packed, LANE), F32),
        in_specs=[
            pl.BlockSpec(memory_space=pl.ANY),
            pl.BlockSpec(memory_space=pltpu.VMEM),
            pl.BlockSpec(memory_space=pltpu.SMEM),
        ],
        out_specs=pl.BlockSpec(memory_space=pltpu.VMEM),
        scratch_shapes=[
            pltpu.VMEM((RING, images, owned, c_in), BF16),
            pltpu.VMEM((c_in, cols), BF16),
            pltpu.VMEM((cols // LANE, images * owned, LANE), F32),
            pltpu.VMEM((RING, owned, rows, images), BF16),
            pltpu.VMEM((RING, rows, 2 * RING * LANE), BF16),
            pltpu.VMEM((RING, packed, LANE), F32),
            pltpu.VMEM((RING, RING, packed // RING, LANE), F32),
            pltpu.VMEM((RING, packed // RING, LANE), F32),
            pltpu.VMEM((RING, packed // RING, LANE), F32),
            dma((RING,)),
            dma((RING, owned)),
            dma((RING, 2 * RING)),
            dma((RING, RING)), dma((RING, RING)),
            dma((RING,)), dma((RING,)),
            dma((RING,)), dma((RING,)),
            dma((RING,)), dma((RING,)),
        ],
        compiler_params=pltpu.CompilerParams(
            collective_id=0, has_side_effects=True, vmem_limit_bytes=56 * 2**20
        ),
        name="pick_and_sum",
    )(features, channel_index, image_counts)
    centres, covars = pl.pallas_call(
        functools.partial(finish_kernel, width),
        out_shape=(
            jax.ShapeDtypeStruct((2, width), F32),
            jax.ShapeDtypeStruct((width, 2, width), F32),
        ),
        in_specs=[pl.BlockSpec(memory_space=pltpu.VMEM)],
        out_specs=(pl.BlockSpec(memory_space=pltpu.VMEM), pl.BlockSpec(memory_space=pltpu.VMEM)),
        compiler_params=pltpu.CompilerParams(vmem_limit_bytes=40 * 2**20),
        name="finish",
    )(tot)
    return centres, jnp.transpose(covars, (1, 0, 2))


def solution(mesh):
    placed = (P(("img", "pos"), None, None), P(), P(("img", "pos")))
    return jax.shard_map(
        body,
        mesh=mesh,
        in_specs=placed,
        out_specs=(P("pos", None), P("pos", None, None)),
        check_vma=False,
    )
```

```python
import functools

import jax
import jax.numpy as jnp
from jax import lax
from jax.experimental import pallas as pl
from jax.experimental.pallas import tpu as pltpu
from jax.sharding import PartitionSpec as P

REG = 0.01
MESH = pl.DeviceIdType.MESH
RING = 4
LANE = 128
F32 = jnp.float32
BF16 = jnp.bfloat16


HEAD = 3 * LANE


def sizes(width):
    rows = -(-(width + 1) // 16) * 16
    full = (width + 1) // LANE // 2 * 2
    strip = -(-(width + 1 - full * LANE) // 8) * 8
    packed = full * full // 2 * LANE + strip * (full + 1) + full // 2
    return rows, full, strip, -(-packed // 32) * 32


def place(i, j, full, strip):
    if i == full:
        return full * full // 2 * LANE + j * strip
    if i == j:
        i = j = i // 2 * 2 + 1
    return (i * (i - 1) // 2 + i // 2 + j) * LANE


def gather_kernel(
    width, feat, chan, count, tot,
    slab, onehot, picked, send, recv, part, half_recv, quarter_recv, owned_sum, b_recv,
    load_sem, send_sem, recv_sem, half_send, half_sem, quarter_send, quarter_sem, b_send, b_sem,
    near_send, near_sem, far_send, far_sem, fw_send, fw_sem,
):
    rows, full, strip, packed = sizes(width)
    images, owned = feat.shape[0], feat.shape[1] // RING
    c_in, cols = onehot.shape
    img, pos = lax.axis_index("img"), lax.axis_index("pos")
    x, c = img // 2, img % 2
    z, y = pos // RING, pos % RING
    ring_b = (1 - c) * y + c * z
    edge = place(3, 0, full, strip)
    spans = ((0, HEAD), (HEAD, rows - HEAD))
    packs = ((0, edge), (edge, packed - edge))

    other, across = x + 1 - 2 * (x % 2), RING - 1 - x
    first_of = (1 - c) * other + c * across
    second_of = (1 - c) * across + c * other

    def share(core):
        return (1 - core) * ((x + 1) // 2 % 2) + core * (x // 2), (1 - core) * (x // 2) + core * (x % 2)

    mine_h, mine_q = share(c)

    barrier = pltpu.get_barrier_semaphore()

    def greet(i, p):
        pl.semaphore_signal(barrier, inc=1, device_id={"img": i, "pos": p}, device_id_type=MESH)

    for d in range(1, RING):
        for k in range(2):
            greet(2 * x + k, (z + d) % RING * RING + y)
            greet(2 * x + k, z * RING + (y + d) % RING)
    greet(2 * other + c, pos)
    greet(2 * across + c, pos)
    greet(2 * x + 1 - c, pos)

    def turn(t):
        return (1 + 2 * t + t // 2) % RING

    def slab_of(t):
        return (z + turn(t)) % RING

    def load(t):
        return pltpu.make_async_copy(
            feat.at[:, pl.ds(slab_of(t) * owned, owned), :], slab.at[t], load_sem.at[t]
        )

    for t in range(RING):
        load(t).start()

    tail = width // LANE * LANE
    onehot[:, tail:] = jnp.zeros((c_in, cols - tail), BF16)
    step = 256

    def build(i, carry):
        at = pl.ds(pl.multiple_of(i * step, step), step)
        which = lax.broadcasted_iota(jnp.int32, (step, width), 0) + i * step
        onehot[at, :width] = jnp.where(which == chan[...].reshape(1, width), 1.0, 0.0).astype(BF16)
        return carry

    lax.fori_loop(0, c_in // step, build, 0)
    last = place(full, full, full, strip)
    for b in range(RING):
        part[b, last:, :] = jnp.zeros((packed - last, LANE), F32)

    usable = lax.broadcasted_iota(jnp.int32, (LANE, images), 1) < count[0]
    is_one = lax.broadcasted_iota(jnp.int32, (LANE, images), 0) == width % LANE
    pl.semaphore_wait(barrier, 4 * (RING - 1) + 3)

    def exchange(n, zp, yp, k):
        to_pos = zp * RING + y if k == 0 else z * RING + yp
        b, a = (yp, z) if k == 0 else (zp, y)
        mine = (c == k) & (to_pos == pos)
        start, height = spans[n]
        src = send.at[zp, 2 * yp + k, start:start + height]
        dst = recv.at[b, start:start + height, pl.ds(pl.multiple_of(a * 2 * LANE + c * LANE, LANE), LANE)]

        @pl.when(mine)
        def _():
            pltpu.make_async_copy(src, dst, recv_sem.at[n, b, a * 2 + c]).start()

        @pl.when(jnp.logical_not(mine))
        def _():
            pltpu.make_async_remote_copy(
                src_ref=src, dst_ref=dst,
                send_sem=send_sem.at[n, zp, 2 * yp + k], recv_sem=recv_sem.at[n, b, a * 2 + c],
                device_id={"img": 2 * x + k, "pos": to_pos}, device_id_type=MESH,
            ).start()

    def pick(t, carry):
        zp = slab_of(t)
        load(t).wait()
        chunk = slab[t].reshape(images * owned, c_in)
        found = jnp.dot(chunk, onehot[...], preferred_element_type=F32)
        for l in range(cols // LANE):
            picked[l] = found[:, l * LANE:(l + 1) * LANE]
        for j in range(owned):
            yp, k = j // 2, j % 2
            for l in range(cols // LANE):
                height = min(LANE, rows - l * LANE)
                block = picked[l, pl.ds(j, images, stride=owned), :].T[:height]
                if l == width // LANE:
                    block = jnp.where(is_one[:height], 1.0, block)
                block = jnp.where(usable[:height], block, 0.0)
                send[zp, j, l * LANE:l * LANE + height, :] = block.astype(BF16)
            if k == 0:
                @pl.when((yp - y + RING) % 2 == 1)
                def _():
                    exchange(0, zp, yp, 0)
            else:
                exchange(0, zp, yp, 1)
        return carry

    lax.fori_loop(0, RING, pick, 0)

    def rest(t, carry):
        exchange(0, slab_of(t % RING), (y + turn(2 + t // RING)) % RING, 0)
        return carry

    lax.fori_loop(0, 2 * RING, rest, 0)

    def second(t, carry):
        d = turn(t % RING)
        exchange(1, (z + d) % RING, (y + turn(t // RING)) % RING, 0)
        exchange(1, slab_of(t // RING), (y + d) % RING, 1)
        return carry

    lax.fori_loop(0, RING * RING, second, 0)

    def half_rows(n, h):
        start, height = packs[n]
        return pl.ds(pl.multiple_of(start + h * (height // 2), 8), height // 2)

    def quarter_rows(n, h, q):
        start, height = packs[n]
        return pl.ds(pl.multiple_of(start + h * (height // 2) + q * (height // 4), 8), height // 4)

    def kept(n, parts):
        start, height = packs[n]
        return pl.ds(start // parts, height // parts)

    def to(chip, core=None):
        return {"img": 2 * chip + (c if core is None else core), "pos": pos}

    def half_copy(n, b):
        return pltpu.make_async_remote_copy(
            src_ref=part.at[b, half_rows(n, 1 - mine_h)], dst_ref=half_recv.at[b, kept(n, 2)],
            send_sem=half_send.at[n, b], recv_sem=half_sem.at[n, b],
            device_id=to(first_of), device_id_type=MESH,
        )

    def quarter_copy(n, b):
        return pltpu.make_async_remote_copy(
            src_ref=part.at[b, quarter_rows(n, mine_h, 1 - mine_q)], dst_ref=quarter_recv.at[b, kept(n, 4)],
            send_sem=quarter_send.at[n, b], recv_sem=quarter_sem.at[n, b],
            device_id=to(second_of), device_id_type=MESH,
        )

    def b_copy(n, b):
        to_pos = (1 - c) * (z * RING + b) + c * (b * RING + y)
        return pltpu.make_async_remote_copy(
            src_ref=owned_sum.at[b, kept(n, 4)], dst_ref=b_recv.at[ring_b, kept(n, 4)],
            send_sem=b_send.at[n, b], recv_sem=b_sem.at[n, ring_b],
            device_id={"img": img, "pos": to_pos}, device_id_type=MESH,
        )

    def near_copy(n):
        at = quarter_rows(n, mine_h, mine_q)
        return pltpu.make_async_remote_copy(
            src_ref=tot.at[c, at], dst_ref=tot.at[c, at], send_sem=near_send.at[n], recv_sem=near_sem.at[n],
            device_id=to(second_of), device_id_type=MESH,
        )

    def far_copy(n):
        at = half_rows(n, mine_h)
        return pltpu.make_async_remote_copy(
            src_ref=tot.at[c, at], dst_ref=tot.at[c, at], send_sem=far_send.at[n], recv_sem=far_sem.at[n],
            device_id=to(first_of), device_id_type=MESH,
        )

    def fw_copy(n, which, core):
        h, q = share(core)
        at = (quarter_rows(n, h, q), quarter_rows(n, h, 1 - q), half_rows(n, 1 - h))[which]
        return pltpu.make_async_remote_copy(
            src_ref=tot.at[core, at], dst_ref=tot.at[core, at],
            send_sem=fw_send.at[n, which], recv_sem=fw_sem.at[n, which],
            device_id=to(x, 1 - c), device_id_type=MESH,
        )

    row = lax.broadcasted_iota(jnp.int32, (LANE, LANE), 0)
    col = lax.broadcasted_iota(jnp.int32, (LANE, LANE), 1)

    def turn_of(t):
        return (ring_b + turn(t)) % RING

    def gram(n, t):
        b = turn_of(t)
        start, height = spans[n]
        for s in range(2 * RING):
            pltpu.make_async_copy(
                send.at[0, 0, start:start + height],
                recv.at[b, start:start + height, s * LANE:(s + 1) * LANE], recv_sem.at[n, b, s],
            ).wait()
        for i in range(HEAD // LANE * n, HEAD // LANE if n == 0 else full + 1):
            tall, wide = (LANE, (i + 1) * LANE) if i < full else (strip, full * LANE + strip)
            prod = lax.dot_general(
                recv[b, i * LANE:i * LANE + tall, :], recv[b, :wide, :],
                (((1,), (1,)), ((), ())), preferred_element_type=F32,
            )
            for j in range(i + 1):
                first = place(i, j, full, strip)
                w = min(LANE, wide - j * LANE)
                block = prod[:, j * LANE:j * LANE + w]
                if i == j and i % 2 == 1:
                    at = place(full, full, full, strip) + strip + i // 2
                    part[b, at:at + 1, :] = jnp.sum(jnp.where(row == col, block, 0.0), axis=0, keepdims=True)
                    block = jnp.where(row >= col, part[b, first:first + LANE, :], block)
                part[b, first:first + tall, :w] = block
        half_copy(n, b).start()

    def settle_half(n, t):
        b = turn_of(t)
        half_copy(n, b).wait_recv()
        at = half_rows(n, mine_h)
        part[b, at] = part[b, at] + half_recv[b, kept(n, 2)]
        quarter_copy(n, b).start()

    def settle_quarter(n, t):
        b = turn_of(t)
        quarter_copy(n, b).wait_recv()
        owned_sum[b, kept(n, 4)] = part[b, quarter_rows(n, mine_h, mine_q)] + quarter_recv[b, kept(n, 4)]

    def total(n):
        found = owned_sum[ring_b, kept(n, 4)]
        for d in (1, 2, 3):
            b = (ring_b + d) % RING
            pltpu.make_async_copy(owned_sum.at[0, kept(n, 4)], b_recv.at[b, kept(n, 4)], b_sem.at[n, b]).wait()
            found = found + b_recv[b, kept(n, 4)]
        tot[c, quarter_rows(n, mine_h, mine_q)] = found
        near_copy(n).start()
        fw_copy(n, 0, c).start()

    def gather_near(n):
        at = quarter_rows(n, mine_h, 1 - mine_q)
        pltpu.make_async_copy(owned_sum.at[0, kept(n, 4)], tot.at[c, at], near_sem.at[n]).wait()
        far_copy(n).start()
        fw_copy(n, 1, c).start()

    def gather_far(n):
        at = half_rows(n, 1 - mine_h)
        pltpu.make_async_copy(half_recv.at[0, kept(n, 2)], tot.at[c, at], far_sem.at[n]).wait()
        fw_copy(n, 2, c).start()

    def first_chunk(t, carry):
        gram(0, t)

        @pl.when(t >= 1)
        def _():
            settle_half(0, t - 1)

        @pl.when(t >= 2)
        def _():
            settle_quarter(0, t - 2)
            b_copy(0, turn_of(t - 2)).start()

        return carry

    lax.fori_loop(0, RING, first_chunk, 0)

    def second_chunk(t, carry):
        gram(1, t)

        @pl.when(t == 0)
        def _():
            settle_half(0, RING - 1)
            settle_quarter(0, RING - 2)
            b_copy(0, turn_of(RING - 2)).start()

        @pl.when(t == 1)
        def _():
            settle_quarter(0, RING - 1)

        @pl.when(t >= 1)
        def _():
            settle_half(1, t - 1)

        @pl.when(t >= 2)
        def _():
            settle_quarter(1, t - 2)
            b_copy(1, turn_of(t - 2)).start()

        @pl.when(t == 2)
        def _():
            total(0)

        @pl.when(t == 3)
        def _():
            gather_near(0)

        return carry

    lax.fori_loop(0, RING, second_chunk, 0)
    settle_half(1, RING - 1)
    settle_quarter(1, RING - 2)
    b_copy(1, turn_of(RING - 2)).start()
    gather_far(0)
    settle_quarter(1, RING - 1)
    total(1)
    gather_near(1)
    gather_far(1)
    for n in range(2):
        for which in range(3):
            fw_copy(n, which, 1 - c).wait_recv()

    def sent(t, carry):
        zp = slab_of(t)
        for j in range(owned):
            yp, k = j // 2, j % 2
            mine = (c == k) & ((zp == z) if k == 0 else (yp == y))

            @pl.when(jnp.logical_not(mine))
            def _():
                for n in range(2):
                    start, height = spans[n]
                    src = send.at[zp, j, start:start + height]
                    pltpu.make_async_copy(src, src, send_sem.at[n, zp, j]).wait()

        return carry

    lax.fori_loop(0, RING, sent, 0)
    for n in range(2):
        for b in range(RING):
            half_copy(n, b).wait_send()
            quarter_copy(n, b).wait_send()
        for d in range(1, RING):
            b_copy(n, (ring_b + d) % RING).wait_send()
        near_copy(n).wait_send()
        far_copy(n).wait_send()
        for which in range(3):
            fw_copy(n, which, c).wait_send()


def finish_kernel(width, tot, centres, covars):
    rows, full, strip, packed = sizes(width)
    row = lax.broadcasted_iota(jnp.int32, (LANE, LANE), 0)
    col = lax.broadcasted_iota(jnp.int32, (LANE, LANE), 1)
    diagonals = place(full, full, full, strip) + strip

    def block(p, i, j):
        first = place(i, j, full, strip)
        if i == full:
            return tot[p, first:first + strip, :]
        both = tot[p, first:first + LANE, :]
        if i > j:
            return both
        if i % 2 == 0:
            return jnp.where(row >= col, both, both.T)
        at = diagonals + i // 2
        return jnp.where(row == col, tot[p, at:at + 1, :], jnp.where(row < col, both, both.T))

    mark = width - full * LANE
    for p in range(tot.shape[0]):
        lin = jnp.concatenate([block(p, full, j)[mark:mark + 1] for j in range(full + 1)], axis=1)
        n = block(p, full, full)[mark:mark + 1, mark:mark + 1]
        centre = lin / n
        centres[p:p + 1, :] = centre[:, :width]
        for i in range(full + 1):
            height = LANE if i < full else strip
            parts = [block(p, i, j) for j in range(i + 1)]
            for j in range(i + 1, full + 1):
                flip = block(p, j, i).T
                if flip.shape[1] < LANE:
                    flip = jnp.concatenate([flip, jnp.zeros((height, LANE - flip.shape[1]), F32)], axis=1)
                parts.append(flip)
            sums = jnp.concatenate(parts, axis=1)
            own = sums[:, width:width + 1] / n
            spread = (sums - n * (own * centre)) / (n - 1.0)
            at = lax.broadcasted_iota(jnp.int32, sums.shape, 0) + i * LANE
            across = lax.broadcasted_iota(jnp.int32, sums.shape, 1)
            spread = spread + jnp.where(at == across, REG, 0.0)
            keep = min(height, width - i * LANE)
            covars[i * LANE:i * LANE + keep, p, :] = spread[:keep, :width]


def body(features, channel_index, image_counts):
    images, positions, c_in = features.shape
    width = channel_index.shape[0]
    rows, full, strip, packed = sizes(width)
    cols = -(-rows // LANE) * LANE
    owned = positions // RING
    dma = pltpu.SemaphoreType.DMA
    tot = pl.pallas_call(
        functools.partial(gather_kernel, width),
        out_shape=jax.ShapeDtypeStruct((2, packed, LANE), F32),
        in_specs=[
            pl.BlockSpec(memory_space=pl.ANY),
            pl.BlockSpec(memory_space=pltpu.VMEM),
            pl.BlockSpec(memory_space=pltpu.SMEM),
        ],
        out_specs=pl.BlockSpec(memory_space=pltpu.VMEM),
        scratch_shapes=[
            pltpu.VMEM((RING, images, owned, c_in), BF16),
            pltpu.VMEM((c_in, cols), BF16),
            pltpu.VMEM((cols // LANE, images * owned, LANE), F32),
            pltpu.VMEM((RING, owned, rows, images), BF16),
            pltpu.VMEM((RING, rows, 2 * RING * LANE), BF16),
            pltpu.VMEM((RING, packed, LANE), F32),
            pltpu.VMEM((RING, packed // 2, LANE), F32),
            pltpu.VMEM((RING, packed // 4, LANE), F32),
            pltpu.VMEM((RING, packed // 4, LANE), F32),
            pltpu.VMEM((RING, packed // 4, LANE), F32),
            dma((RING,)),
            dma((2, RING, owned)),
            dma((2, RING, 2 * RING)),
            dma((2, RING)), dma((2, RING)),
            dma((2, RING)), dma((2, RING)),
            dma((2, RING)), dma((2, RING)),
            dma((2,)), dma((2,)),
            dma((2,)), dma((2,)),
            dma((2, 3)), dma((2, 3)),
        ],
        compiler_params=pltpu.CompilerParams(
            collective_id=0, has_side_effects=True, vmem_limit_bytes=56 * 2**20
        ),
        name="pick_and_sum",
    )(features, channel_index, image_counts)
    centres, covars = pl.pallas_call(
        functools.partial(finish_kernel, width),
        out_shape=(
            jax.ShapeDtypeStruct((2, width), F32),
            jax.ShapeDtypeStruct((width, 2, width), F32),
        ),
        in_specs=[pl.BlockSpec(memory_space=pltpu.VMEM)],
        out_specs=(pl.BlockSpec(memory_space=pltpu.VMEM), pl.BlockSpec(memory_space=pltpu.VMEM)),
        compiler_params=pltpu.CompilerParams(vmem_limit_bytes=40 * 2**20),
        name="finish",
    )(tot)
    return centres, jnp.transpose(covars, (1, 0, 2))


def solution(mesh):
    placed = (P(("img", "pos"), None, None), P(), P(("img", "pos")))
    return jax.shard_map(
        body,
        mesh=mesh,
        in_specs=placed,
        out_specs=(P("pos", None), P("pos", None, None)),
        check_vma=False,
    )
```

```python
import functools

import jax
import jax.numpy as jnp
from jax import lax
from jax.experimental import pallas as pl
from jax.experimental.pallas import tpu as pltpu
from jax.sharding import PartitionSpec as P

REG = 0.01
MESH = pl.DeviceIdType.MESH
RING = 4
LANE = 128
F32 = jnp.float32
BF16 = jnp.bfloat16


def sizes(width):
    rows = -(-(width + 1) // 16) * 16
    full = (width + 1) // LANE // 2 * 2
    strip = -(-(width + 1 - full * LANE) // 8) * 8
    packed = full * full // 2 * LANE + strip * (full + 1) + full // 2
    return rows, full, strip, -(-packed // 32) * 32


def place(i, j, full, strip):
    if i == full:
        return full * full // 2 * LANE + j * strip
    if i == j:
        return (full * (full - 1) // 2 + i // 2) * LANE
    return (i * (i - 1) // 2 + j) * LANE


def gather_kernel(
    width, feat, chan, count, tot,
    slab, onehot, picked, send, recv, part, x_recv, owned_sum, b_recv,
    load_sem, send_sem, recv_sem, x_send, x_sem, b_send, b_sem, ag_send, ag_sem, fw_send, fw_sem,
):
    rows, full, strip, packed = sizes(width)
    piece = packed // RING
    images, owned = feat.shape[0], feat.shape[1] // RING
    c_in, cols = onehot.shape
    img, pos = lax.axis_index("img"), lax.axis_index("pos")
    x, c = img // 2, img % 2
    z, y = pos // RING, pos % RING
    ring_b = (1 - c) * y + c * z

    barrier = pltpu.get_barrier_semaphore()

    def greet(i, p):
        pl.semaphore_signal(barrier, inc=1, device_id={"img": i, "pos": p}, device_id_type=MESH)

    for d in range(1, RING):
        for k in range(2):
            greet(2 * x + k, (z + d) % RING * RING + y)
            greet(2 * x + k, z * RING + (y + d) % RING)
        greet((x + d) % RING * 2 + c, pos)
    greet(2 * x + 1 - c, pos)

    def turn(t):
        return (1 + 2 * t + t // 2) % RING

    def slab_of(t):
        return (z + turn(t)) % RING

    def load(t):
        return pltpu.make_async_copy(
            feat.at[:, pl.ds(slab_of(t) * owned, owned), :], slab.at[t], load_sem.at[t]
        )

    for t in range(RING):
        load(t).start()

    tail = width // LANE * LANE
    onehot[:, tail:] = jnp.zeros((c_in, cols - tail), BF16)
    step = 256

    def build(i, carry):
        at = pl.ds(pl.multiple_of(i * step, step), step)
        which = lax.broadcasted_iota(jnp.int32, (step, width), 0) + i * step
        onehot[at, :width] = jnp.where(which == chan[...].reshape(1, width), 1.0, 0.0).astype(BF16)
        return carry

    lax.fori_loop(0, c_in // step, build, 0)
    last = place(full, full, full, strip)
    for b in range(RING):
        part[b, last:, :] = jnp.zeros((packed - last, LANE), F32)

    usable = lax.broadcasted_iota(jnp.int32, (LANE, images), 1) < count[0]
    is_one = lax.broadcasted_iota(jnp.int32, (LANE, images), 0) == width % LANE
    pl.semaphore_wait(barrier, 5 * (RING - 1) + 1)

    def exchange(zp, yp, k):
        to_pos = zp * RING + y if k == 0 else z * RING + yp
        b, a = (yp, z) if k == 0 else (zp, y)
        mine = (c == k) & (to_pos == pos)
        src = send.at[zp, 2 * yp + k]
        dst = recv.at[b, :, pl.ds(pl.multiple_of(a * 2 * LANE + c * LANE, LANE), LANE)]

        @pl.when(mine)
        def _():
            pltpu.make_async_copy(src, dst, recv_sem.at[b, a * 2 + c]).start()

        @pl.when(jnp.logical_not(mine))
        def _():
            pltpu.make_async_remote_copy(
                src_ref=src, dst_ref=dst,
                send_sem=send_sem.at[zp, 2 * yp + k], recv_sem=recv_sem.at[b, a * 2 + c],
                device_id={"img": 2 * x + k, "pos": to_pos}, device_id_type=MESH,
            ).start()

    def rows_of(q):
        return pl.ds(pl.multiple_of(q * piece, 8), piece)

    def x_copy(b, d):
        q = (x + d) % RING
        return pltpu.make_async_remote_copy(
            src_ref=part.at[b, rows_of(q)], dst_ref=x_recv.at[b, x],
            send_sem=x_send.at[b, q], recv_sem=x_sem.at[b, x],
            device_id={"img": 2 * q + c, "pos": pos}, device_id_type=MESH,
        )

    def b_copy(b):
        to_pos = (1 - c) * (z * RING + b) + c * (b * RING + y)
        return pltpu.make_async_remote_copy(
            src_ref=owned_sum.at[b], dst_ref=b_recv.at[ring_b],
            send_sem=b_send.at[b], recv_sem=b_sem.at[ring_b],
            device_id={"img": img, "pos": to_pos}, device_id_type=MESH,
        )

    row = lax.broadcasted_iota(jnp.int32, (LANE, LANE), 0)
    col = lax.broadcasted_iota(jnp.int32, (LANE, LANE), 1)

    def gram(t):
        b = (ring_b + turn(t)) % RING
        for s in range(2 * RING):
            pltpu.make_async_copy(
                send.at[0, 0], recv.at[b, :, s * LANE:(s + 1) * LANE], recv_sem.at[b, s]
            ).wait()
        for i in range(full + 1):
            height, wide = (LANE, (i + 1) * LANE) if i < full else (strip, full * LANE + strip)
            prod = lax.dot_general(
                recv[b, i * LANE:i * LANE + height, :], recv[b, :wide, :],
                (((1,), (1,)), ((), ())), preferred_element_type=F32,
            )
            for j in range(i + 1):
                first = place(i, j, full, strip)
                w = min(LANE, wide - j * LANE)
                block = prod[:, j * LANE:j * LANE + w]
                if i == j and i % 2 == 1:
                    at = place(full, full, full, strip) + strip + i // 2
                    part[b, at:at + 1, :] = jnp.sum(jnp.where(row == col, block, 0.0), axis=0, keepdims=True)
                    block = jnp.where(row >= col, part[b, first:first + LANE, :], block)
                part[b, first:first + height, :w] = block
        for d in (2, 1, 3):
            x_copy(b, d).start()

    def settle(t):
        b = (ring_b + turn(t)) % RING
        total = part[b, rows_of(x)]
        for d in (1, 3, 2):
            q = (x + d) % RING
            pltpu.make_async_copy(owned_sum.at[0], x_recv.at[b, q], x_sem.at[b, q]).wait()
            total = total + x_recv[b, q]
        owned_sum[b] = total

    def pick(t, carry):
        zp = slab_of(t)
        load(t).wait()
        group = images

        def multiply(g, carry):
            at = pl.ds(pl.multiple_of(g * group, group), group)
            chunk = slab[t, at].reshape(group * owned, c_in)
            to = pl.ds(pl.multiple_of(g * group * owned, group * owned), group * owned)
            found = jnp.dot(chunk, onehot[...], preferred_element_type=F32)
            for l in range(cols // LANE):
                picked[l, to, :] = found[:, l * LANE:(l + 1) * LANE]
            return carry

        lax.fori_loop(0, images // group, multiply, 0)
        for j in range(owned):
            for l in range(cols // LANE):
                height = min(LANE, rows - l * LANE)
                block = picked[l, pl.ds(j, images, stride=owned), :].T[:height]
                if l == width // LANE:
                    block = jnp.where(is_one[:height], 1.0, block)
                block = jnp.where(usable[:height], block, 0.0)
                send[zp, j, l * LANE:l * LANE + height, :] = block.astype(BF16)
        for d in (1, 3, 2, 0):
            exchange(zp, (y + d) % RING, 1)
            if d == 1 or d == 3:
                exchange(zp, (y + d) % RING, 0)

        @pl.when((c == 1) & (t == 2))
        def _():
            gram(0)

        return carry

    lax.fori_loop(0, RING, pick, 0)

    def rest(t, carry):
        exchange(slab_of(t % RING), (y + turn(2 + t // RING)) % RING, 0)
        return carry

    lax.fori_loop(0, 2 * RING, rest, 0)

    @pl.when(c == 0)
    def _():
        gram(0)

    def stage(t, carry):
        gram(t)
        settle(t - 1)
        b_copy((ring_b + turn(t - 1)) % RING).start()
        return carry

    lax.fori_loop(1, RING, stage, 0)
    settle(RING - 1)

    def ag_copy(d):
        q = (x + d) % RING
        return pltpu.make_async_remote_copy(
            src_ref=tot.at[c, rows_of(x)], dst_ref=tot.at[c, rows_of(x)],
            send_sem=ag_send.at[q], recv_sem=ag_sem.at[x],
            device_id={"img": 2 * q + c, "pos": pos}, device_id_type=MESH,
        )

    def fw_copy(q):
        return pltpu.make_async_remote_copy(
            src_ref=tot.at[c, rows_of(q)], dst_ref=tot.at[c, rows_of(q)],
            send_sem=fw_send.at[q], recv_sem=fw_sem.at[q],
            device_id={"img": 2 * x + 1 - c, "pos": pos}, device_id_type=MESH,
        )

    total = owned_sum[ring_b]
    for d in (1, 2, 3):
        b = (ring_b + d) % RING
        pltpu.make_async_copy(owned_sum.at[0], b_recv.at[b], b_sem.at[b]).wait()
        total = total + b_recv[b]
    tot[c, rows_of(x)] = total
    for d in (2, 1, 3):
        ag_copy(d).start()
    fw_copy(x).start()
    for d in (1, 3, 2):
        q = (x + d) % RING
        pltpu.make_async_copy(owned_sum.at[0], tot.at[c, rows_of(q)], ag_sem.at[q]).wait()
        fw_copy(q).start()
    for q in range(RING):
        pltpu.make_async_copy(owned_sum.at[0], tot.at[1 - c, rows_of(q)], fw_sem.at[q]).wait()

    def sent(t, carry):
        zp = slab_of(t)
        for j in range(owned):
            yp, k = j // 2, j % 2
            mine = (c == k) & ((zp == z) if k == 0 else (yp == y))

            @pl.when(jnp.logical_not(mine))
            def _():
                pltpu.make_async_copy(send.at[zp, j], send.at[zp, j], send_sem.at[zp, j]).wait()

        return carry

    lax.fori_loop(0, RING, sent, 0)
    for d in range(1, RING):
        b_copy((ring_b + d) % RING).wait_send()
        for b in range(RING):
            x_copy(b, d).wait_send()
        ag_copy(d).wait_send()
    for q in range(RING):
        fw_copy(q).wait_send()


def finish_kernel(width, tot, centres, covars):
    rows, full, strip, packed = sizes(width)
    row = lax.broadcasted_iota(jnp.int32, (LANE, LANE), 0)
    col = lax.broadcasted_iota(jnp.int32, (LANE, LANE), 1)
    diagonals = place(full, full, full, strip) + strip

    def block(p, i, j):
        first = place(i, j, full, strip)
        if i == full:
            return tot[p, first:first + strip, :]
        both = tot[p, first:first + LANE, :]
        if i > j:
            return both
        if i % 2 == 0:
            return jnp.where(row >= col, both, both.T)
        at = diagonals + i // 2
        return jnp.where(row == col, tot[p, at:at + 1, :], jnp.where(row < col, both, both.T))

    mark = width - full * LANE
    for p in range(tot.shape[0]):
        lin = jnp.concatenate([block(p, full, j)[mark:mark + 1] for j in range(full + 1)], axis=1)
        n = block(p, full, full)[mark:mark + 1, mark:mark + 1]
        centre = lin / n
        centres[p:p + 1, :] = centre[:, :width]
        for i in range(full + 1):
            height = LANE if i < full else strip
            parts = [block(p, i, j) for j in range(i + 1)]
            for j in range(i + 1, full + 1):
                flip = block(p, j, i).T
                if flip.shape[1] < LANE:
                    flip = jnp.concatenate([flip, jnp.zeros((height, LANE - flip.shape[1]), F32)], axis=1)
                parts.append(flip)
            sums = jnp.concatenate(parts, axis=1)
            own = sums[:, width:width + 1] / n
            spread = (sums - n * (own * centre)) / (n - 1.0)
            at = lax.broadcasted_iota(jnp.int32, sums.shape, 0) + i * LANE
            across = lax.broadcasted_iota(jnp.int32, sums.shape, 1)
            spread = spread + jnp.where(at == across, REG, 0.0)
            keep = min(height, width - i * LANE)
            covars[i * LANE:i * LANE + keep, p, :] = spread[:keep, :width]


def body(features, channel_index, image_counts):
    images, positions, c_in = features.shape
    width = channel_index.shape[0]
    rows, full, strip, packed = sizes(width)
    cols = -(-rows // LANE) * LANE
    owned = positions // RING
    dma = pltpu.SemaphoreType.DMA
    tot = pl.pallas_call(
        functools.partial(gather_kernel, width),
        out_shape=pltpu.VMEM((2, packed, LANE), F32),
        in_specs=[
            pl.BlockSpec(memory_space=pl.ANY),
            pl.BlockSpec(memory_space=pltpu.VMEM),
            pl.BlockSpec(memory_space=pltpu.SMEM),
        ],
        out_specs=pl.BlockSpec(memory_space=pltpu.VMEM),
        scratch_shapes=[
            pltpu.VMEM((RING, images, owned, c_in), BF16),
            pltpu.VMEM((c_in, cols), BF16),
            pltpu.VMEM((cols // LANE, images * owned, LANE), F32),
            pltpu.VMEM((RING, owned, rows, images), BF16),
            pltpu.VMEM((RING, rows, 2 * RING * LANE), BF16),
            pltpu.VMEM((RING, packed, LANE), F32),
            pltpu.VMEM((RING, RING, packed // RING, LANE), F32),
            pltpu.VMEM((RING, packed // RING, LANE), F32),
            pltpu.VMEM((RING, packed // RING, LANE), F32),
            dma((RING,)),
            dma((RING, owned)),
            dma((RING, 2 * RING)),
            dma((RING, RING)), dma((RING, RING)),
            dma((RING,)), dma((RING,)),
            dma((RING,)), dma((RING,)),
            dma((RING,)), dma((RING,)),
        ],
        compiler_params=pltpu.CompilerParams(
            collective_id=0, has_side_effects=True, vmem_limit_bytes=56 * 2**20
        ),
        name="pick_and_sum",
    )(features, channel_index, image_counts)
    centres, covars = pl.pallas_call(
        functools.partial(finish_kernel, width),
        out_shape=(
            jax.ShapeDtypeStruct((2, width), F32),
            jax.ShapeDtypeStruct((width, 2, width), F32),
        ),
        in_specs=[pl.BlockSpec(memory_space=pltpu.VMEM)],
        out_specs=(pl.BlockSpec(memory_space=pltpu.VMEM), pl.BlockSpec(memory_space=pltpu.VMEM)),
        compiler_params=pltpu.CompilerParams(vmem_limit_bytes=40 * 2**20),
        name="finish",
    )(tot)
    return centres, jnp.transpose(covars, (1, 0, 2))


def solution(mesh):
    placed = (P(("img", "pos"), None, None), P(), P(("img", "pos")))
    return jax.shard_map(
        body,
        mesh=mesh,
        in_specs=placed,
        out_specs=(P("pos", None), P("pos", None, None)),
        check_vma=False,
    )
```

```python
import functools

import jax
import jax.numpy as jnp
from jax import lax
from jax.experimental import pallas as pl
from jax.experimental.pallas import tpu as pltpu
from jax.sharding import PartitionSpec as P

REG = 0.01
MESH = pl.DeviceIdType.MESH
RING = 4
LANE = 128
F32 = jnp.float32
BF16 = jnp.bfloat16


def sizes(width):
    rows = -(-(width + 1) // 16) * 16
    full = (width + 1) // LANE // 2 * 2
    strip = -(-(width + 1 - full * LANE) // 8) * 8
    packed = full * full // 2 * LANE + strip * (full + 1) + full // 2
    return rows, full, strip, -(-packed // 32) * 32


def place(i, j, full, strip):
    if i == full:
        return full * full // 2 * LANE + j * strip
    if i == j:
        return (full * (full - 1) // 2 + i // 2) * LANE
    return (i * (i - 1) // 2 + j) * LANE


def gather_kernel(
    width, feat, chan, count, tot,
    slab, onehot, picked, send, recv, part, x_recv, owned_sum, b_recv,
    load_sem, send_sem, recv_sem, x_send, x_sem, b_send, b_sem, ag_send, ag_sem, fw_send, fw_sem,
):
    rows, full, strip, packed = sizes(width)
    piece = packed // RING
    images, owned = feat.shape[0], feat.shape[1] // RING
    c_in, cols = onehot.shape
    img, pos = lax.axis_index("img"), lax.axis_index("pos")
    x, c = img // 2, img % 2
    z, y = pos // RING, pos % RING
    ring_b = (1 - c) * y + c * z

    def turn(t):
        return (1 + 2 * t + t // 2) % RING

    def slab_of(t):
        return (z + turn(t)) % RING

    def load(t):
        return pltpu.make_async_copy(
            feat.at[:, pl.ds(slab_of(t) * owned, owned), :], slab.at[t], load_sem.at[t]
        )

    for t in range(RING):
        load(t).start()

    barrier = pltpu.get_barrier_semaphore()

    def greet(i, p):
        pl.semaphore_signal(barrier, inc=1, device_id={"img": i, "pos": p}, device_id_type=MESH)

    for d in range(1, RING):
        for k in range(2):
            greet(2 * x + k, (z + d) % RING * RING + y)
            greet(2 * x + k, z * RING + (y + d) % RING)
        greet((x + d) % RING * 2 + c, pos)
    greet(2 * x + 1 - c, pos)

    tail = width // LANE * LANE
    onehot[:, tail:] = jnp.zeros((c_in, cols - tail), BF16)
    step = 256

    def build(i, carry):
        at = pl.ds(pl.multiple_of(i * step, step), step)
        which = lax.broadcasted_iota(jnp.int32, (step, width), 0) + i * step
        onehot[at, :width] = jnp.where(which == chan[...].reshape(1, width), 1.0, 0.0).astype(BF16)
        return carry

    lax.fori_loop(0, c_in // step, build, 0)
    last = place(full, full, full, strip)
    for b in range(RING):
        part[b, last:, :] = jnp.zeros((packed - last, LANE), F32)

    usable = lax.broadcasted_iota(jnp.int32, (LANE, images), 1) < count[0]
    is_one = lax.broadcasted_iota(jnp.int32, (LANE, images), 0) == width % LANE

    def exchange(zp, yp, k):
        to_pos = zp * RING + y if k == 0 else z * RING + yp
        b, a = (yp, z) if k == 0 else (zp, y)
        mine = (c == k) & (to_pos == pos)
        src = send.at[zp, 2 * yp + k]
        dst = recv.at[b, :, pl.ds(pl.multiple_of(a * 2 * LANE + c * LANE, LANE), LANE)]

        @pl.when(mine)
        def _():
            pltpu.make_async_copy(src, dst, recv_sem.at[b, a * 2 + c]).start()

        @pl.when(jnp.logical_not(mine))
        def _():
            pltpu.make_async_remote_copy(
                src_ref=src, dst_ref=dst,
                send_sem=send_sem.at[zp, 2 * yp + k], recv_sem=recv_sem.at[b, a * 2 + c],
                device_id={"img": 2 * x + k, "pos": to_pos}, device_id_type=MESH,
            ).start()

    def rows_of(q):
        return pl.ds(pl.multiple_of(q * piece, 8), piece)

    def x_copy(b, d):
        q = (x + d) % RING
        return pltpu.make_async_remote_copy(
            src_ref=part.at[b, rows_of(q)], dst_ref=x_recv.at[b, x],
            send_sem=x_send.at[b, q], recv_sem=x_sem.at[b, x],
            device_id={"img": 2 * q + c, "pos": pos}, device_id_type=MESH,
        )

    def b_copy(b):
        to_pos = (1 - c) * (z * RING + b) + c * (b * RING + y)
        return pltpu.make_async_remote_copy(
            src_ref=owned_sum.at[b], dst_ref=b_recv.at[ring_b],
            send_sem=b_send.at[b], recv_sem=b_sem.at[ring_b],
            device_id={"img": img, "pos": to_pos}, device_id_type=MESH,
        )

    row = lax.broadcasted_iota(jnp.int32, (LANE, LANE), 0)
    col = lax.broadcasted_iota(jnp.int32, (LANE, LANE), 1)

    def arrive(t):
        b = (ring_b + turn(t)) % RING
        for s in range(2 * RING):
            pltpu.make_async_copy(
                send.at[0, 0], recv.at[b, :, s * LANE:(s + 1) * LANE], recv_sem.at[b, s]
            ).wait()

    def gram(t):
        b = (ring_b + turn(t)) % RING
        for i in range(full + 1):
            height, wide = (LANE, (i + 1) * LANE) if i < full else (strip, full * LANE + strip)
            prod = lax.dot_general(
                recv[b, i * LANE:i * LANE + height, :], recv[b, :wide, :],
                (((1,), (1,)), ((), ())), preferred_element_type=F32,
            )
            for j in range(i + 1):
                first = place(i, j, full, strip)
                w = min(LANE, wide - j * LANE)
                block = prod[:, j * LANE:j * LANE + w]
                if i == j and i % 2 == 1:
                    at = place(full, full, full, strip) + strip + i // 2
                    part[b, at:at + 1, :] = jnp.sum(jnp.where(row == col, block, 0.0), axis=0, keepdims=True)
                    block = jnp.where(row >= col, part[b, first:first + LANE, :], block)
                part[b, first:first + height, :w] = block
        for d in (2, 1, 3):
            x_copy(b, d).start()

    def settle(t):
        b = (ring_b + turn(t)) % RING
        total = part[b, rows_of(x)]
        for d in (1, 3, 2):
            q = (x + d) % RING
            pltpu.make_async_copy(owned_sum.at[0], x_recv.at[b, q], x_sem.at[b, q]).wait()
            total = total + x_recv[b, q]
        owned_sum[b] = total

    def pick(t):
        zp = slab_of(t)
        load(t).wait()
        group = images

        def multiply(g, carry):
            at = pl.ds(pl.multiple_of(g * group, group), group)
            chunk = slab[t, at].reshape(group * owned, c_in)
            to = pl.ds(pl.multiple_of(g * group * owned, group * owned), group * owned)
            found = jnp.dot(chunk, onehot[...], preferred_element_type=F32)
            for l in range(cols // LANE):
                picked[l, to, :] = found[:, l * LANE:(l + 1) * LANE]
            return carry

        lax.fori_loop(0, images // group, multiply, 0)
        for j in range(owned):
            for l in range(cols // LANE):
                height = min(LANE, rows - l * LANE)
                block = picked[l, pl.ds(j, images, stride=owned), :].T[:height]
                if l == width // LANE:
                    block = jnp.where(is_one[:height], 1.0, block)
                block = jnp.where(usable[:height], block, 0.0)
                send[zp, j, l * LANE:l * LANE + height, :] = block.astype(BF16)

    def offer(t):
        zp = slab_of(t)
        for d in (1, 3):
            exchange(zp, (y + d) % RING, 0)

        @pl.when(t < 2)
        def _():
            for d in (1, 3, 2, 0):
                exchange(zp, (y + d) % RING, 1)

    def next_slab(t, carry):
        pick(t)
        offer(t)
        return carry

    pick(0)
    pl.semaphore_wait(barrier, 5 * (RING - 1) + 1)
    offer(0)
    lax.fori_loop(1, RING, next_slab, 0)

    def later(n):
        def one(i, carry):
            d = turn(i)
            exchange((z + d) % RING, (y + turn(n)) % RING, 0)
            exchange(slab_of(n), (y + d) % RING, 1)
            return carry

        lax.fori_loop(0, RING, one, 0)

    arrive(0)
    later(2)
    gram(0)

    def stage(t, carry):
        arrive(t)

        @pl.when(t == 1)
        def _():
            later(3)

        gram(t)
        settle(t - 1)
        b_copy((ring_b + turn(t - 1)) % RING).start()
        return carry

    lax.fori_loop(1, RING, stage, 0)
    settle(RING - 1)

    def ag_copy(d):
        q = (x + d) % RING
        return pltpu.make_async_remote_copy(
            src_ref=tot.at[c, rows_of(x)], dst_ref=tot.at[c, rows_of(x)],
            send_sem=ag_send.at[q], recv_sem=ag_sem.at[x],
            device_id={"img": 2 * q + c, "pos": pos}, device_id_type=MESH,
        )

    def fw_copy(q):
        return pltpu.make_async_remote_copy(
            src_ref=tot.at[c, rows_of(q)], dst_ref=tot.at[c, rows_of(q)],
            send_sem=fw_send.at[q], recv_sem=fw_sem.at[q],
            device_id={"img": 2 * x + 1 - c, "pos": pos}, device_id_type=MESH,
        )

    total = owned_sum[ring_b]
    for d in (1, 2, 3):
        b = (ring_b + d) % RING
        pltpu.make_async_copy(owned_sum.at[0], b_recv.at[b], b_sem.at[b]).wait()
        total = total + b_recv[b]
    tot[c, rows_of(x)] = total
    for d in (2, 1, 3):
        ag_copy(d).start()
    fw_copy(x).start()
    for d in (1, 3, 2):
        q = (x + d) % RING
        pltpu.make_async_copy(owned_sum.at[0], tot.at[c, rows_of(q)], ag_sem.at[q]).wait()
        fw_copy(q).start()
    for q in range(RING):
        pltpu.make_async_copy(owned_sum.at[0], tot.at[1 - c, rows_of(q)], fw_sem.at[q]).wait()

    def sent(t, carry):
        zp = slab_of(t)
        for j in range(owned):
            yp, k = j // 2, j % 2
            mine = (c == k) & ((zp == z) if k == 0 else (yp == y))

            @pl.when(jnp.logical_not(mine))
            def _():
                pltpu.make_async_copy(send.at[zp, j], send.at[zp, j], send_sem.at[zp, j]).wait()

        return carry

    lax.fori_loop(0, RING, sent, 0)
    for d in range(1, RING):
        b_copy((ring_b + d) % RING).wait_send()
        for b in range(RING):
            x_copy(b, d).wait_send()
        ag_copy(d).wait_send()
    for q in range(RING):
        fw_copy(q).wait_send()


def finish_kernel(width, tot, centres, covars, made, sem):
    rows, full, strip, packed = sizes(width)
    row = lax.broadcasted_iota(jnp.int32, (LANE, LANE), 0)
    col = lax.broadcasted_iota(jnp.int32, (LANE, LANE), 1)
    diagonals = place(full, full, full, strip) + strip

    def block(p, i, j):
        first = place(i, j, full, strip)
        if i == full:
            return tot[p, first:first + strip, :]
        both = tot[p, first:first + LANE, :]
        if i > j:
            return both
        if i % 2 == 0:
            return jnp.where(row >= col, both, both.T)
        at = diagonals + i // 2
        return jnp.where(row == col, tot[p, at:at + 1, :], jnp.where(row < col, both, both.T))

    mark = width - full * LANE
    copies, means = [], []
    for p in range(tot.shape[0]):
        lin = jnp.concatenate([block(p, full, j)[mark:mark + 1] for j in range(full + 1)], axis=1)
        n = block(p, full, full)[mark:mark + 1, mark:mark + 1]
        means.append((n, lin / n))
        centres[p:p + 1, :] = means[p][1][:, :width]
    for i in range(full + 1):
        height = LANE if i < full else strip
        keep = min(height, width - i * LANE)
        for p in range(tot.shape[0]):
            n, centre = means[p]
            parts = [block(p, i, j) for j in range(i + 1)]
            for j in range(i + 1, full + 1):
                flip = block(p, j, i).T
                if flip.shape[1] < LANE:
                    flip = jnp.concatenate([flip, jnp.zeros((height, LANE - flip.shape[1]), F32)], axis=1)
                parts.append(flip)
            sums = jnp.concatenate(parts, axis=1)
            own = sums[:, width:width + 1] / n
            spread = (sums - n * (own * centre)) / (n - 1.0)
            at = lax.broadcasted_iota(jnp.int32, sums.shape, 0) + i * LANE
            across = lax.broadcasted_iota(jnp.int32, sums.shape, 1)
            spread = spread + jnp.where(at == across, REG, 0.0)
            made[i * LANE:i * LANE + keep, p, :] = spread[:keep, :width]
        rows_made = slice(i * LANE, i * LANE + keep)
        copies.append(pltpu.make_async_copy(made.at[rows_made], covars.at[rows_made], sem.at[i]))
        copies[-1].start()
    for copy in copies:
        copy.wait()


def body(features, channel_index, image_counts):
    images, positions, c_in = features.shape
    width = channel_index.shape[0]
    rows, full, strip, packed = sizes(width)
    cols = -(-rows // LANE) * LANE
    owned = positions // RING
    dma = pltpu.SemaphoreType.DMA
    tot = pl.pallas_call(
        functools.partial(gather_kernel, width),
        out_shape=pltpu.VMEM((2, packed, LANE), F32),
        in_specs=[
            pl.BlockSpec(memory_space=pl.ANY),
            pl.BlockSpec(memory_space=pltpu.VMEM),
            pl.BlockSpec(memory_space=pltpu.SMEM),
        ],
        out_specs=pl.BlockSpec(memory_space=pltpu.VMEM),
        scratch_shapes=[
            pltpu.VMEM((RING, images, owned, c_in), BF16),
            pltpu.VMEM((c_in, cols), BF16),
            pltpu.VMEM((cols // LANE, images * owned, LANE), F32),
            pltpu.VMEM((RING, owned, rows, images), BF16),
            pltpu.VMEM((RING, rows, 2 * RING * LANE), BF16),
            pltpu.VMEM((RING, packed, LANE), F32),
            pltpu.VMEM((RING, RING, packed // RING, LANE), F32),
            pltpu.VMEM((RING, packed // RING, LANE), F32),
            pltpu.VMEM((RING, packed // RING, LANE), F32),
            dma((RING,)),
            dma((RING, owned)),
            dma((RING, 2 * RING)),
            dma((RING, RING)), dma((RING, RING)),
            dma((RING,)), dma((RING,)),
            dma((RING,)), dma((RING,)),
            dma((RING,)), dma((RING,)),
        ],
        compiler_params=pltpu.CompilerParams(
            collective_id=0, has_side_effects=True, vmem_limit_bytes=56 * 2**20
        ),
        name="pick_and_sum",
    )(features, channel_index, image_counts)
    centres, covars = pl.pallas_call(
        functools.partial(finish_kernel, width),
        out_shape=(
            jax.ShapeDtypeStruct((2, width), F32),
            jax.ShapeDtypeStruct((width, 2, width), F32),
        ),
        in_specs=[pl.BlockSpec(memory_space=pltpu.VMEM)],
        out_specs=(pl.BlockSpec(memory_space=pltpu.VMEM), pl.BlockSpec(memory_space=pl.ANY)),
        scratch_shapes=[pltpu.VMEM((width, 2, width), F32), dma((full + 1,))],
        compiler_params=pltpu.CompilerParams(vmem_limit_bytes=40 * 2**20),
        name="finish",
    )(tot)
    return centres, jnp.transpose(covars, (1, 0, 2))


def solution(mesh):
    placed = (P(("img", "pos"), None, None), P(), P(("img", "pos")))
    return jax.shard_map(
        body,
        mesh=mesh,
        in_specs=placed,
        out_specs=(P("pos", None), P("pos", None, None)),
        check_vma=False,
    )
```

```python
import functools

import jax
import jax.numpy as jnp
from jax import lax
from jax.experimental import pallas as pl
from jax.experimental.pallas import tpu as pltpu
from jax.sharding import PartitionSpec as P

REG = 0.01
MESH = pl.DeviceIdType.MESH
RING = 4
LANE = 128
F32 = jnp.float32
BF16 = jnp.bfloat16


def sizes(width):
    rows = -(-(width + 1) // 16) * 16
    full = (width + 1) // LANE // 2 * 2
    strip = -(-(width + 1 - full * LANE) // 8) * 8
    packed = full * full // 2 * LANE + strip * (full + 1) + full // 2
    return rows, full, strip, -(-packed // 32) * 32


def place(i, j, full, strip):
    if i == full:
        return full * full // 2 * LANE + j * strip
    if i == j:
        return (full * (full - 1) // 2 + i // 2) * LANE
    return (i * (i - 1) // 2 + j) * LANE


def gather_kernel(
    width, feat, chan, count, tot,
    slab, onehot, picked, send, recv, part, x_recv, owned_sum, b_recv,
    load_sem, send_sem, recv_sem, x_send, x_sem, b_send, b_sem, ag_send, ag_sem, fw_send, fw_sem,
):
    rows, full, strip, packed = sizes(width)
    piece = packed // RING
    images, owned = feat.shape[0], feat.shape[1] // RING
    c_in, cols = onehot.shape
    img, pos = lax.axis_index("img"), lax.axis_index("pos")
    x, c = img // 2, img % 2
    z, y = pos // RING, pos % RING
    ring_b = (1 - c) * y + c * z

    def turn(t):
        return (1 + 2 * t + t // 2) % RING

    def slab_of(t):
        return (z + turn(t)) % RING

    def load(t):
        return pltpu.make_async_copy(
            feat.at[:, pl.ds(slab_of(t) * owned, owned), :], slab.at[t], load_sem.at[t]
        )

    for t in range(RING):
        load(t).start()

    barrier = pltpu.get_barrier_semaphore()

    def greet(i, p):
        pl.semaphore_signal(barrier, inc=1, device_id={"img": i, "pos": p}, device_id_type=MESH)

    for d in range(1, RING):
        for k in range(2):
            greet(2 * x + k, (z + d) % RING * RING + y)
            greet(2 * x + k, z * RING + (y + d) % RING)
        greet((x + d) % RING * 2 + c, pos)
    greet(2 * x + 1 - c, pos)

    tail = width // LANE * LANE
    onehot[:, tail:] = jnp.zeros((c_in, cols - tail), BF16)
    step = 256

    def build(i, carry):
        at = pl.ds(pl.multiple_of(i * step, step), step)
        which = lax.broadcasted_iota(jnp.int32, (step, width), 0) + i * step
        onehot[at, :width] = jnp.where(which == chan[...].reshape(1, width), 1.0, 0.0).astype(BF16)
        return carry

    lax.fori_loop(0, c_in // step, build, 0)
    last = place(full, full, full, strip)
    for b in range(RING):
        part[b, last:, :] = jnp.zeros((packed - last, LANE), F32)

    usable = lax.broadcasted_iota(jnp.int32, (LANE, images), 1) < count[0]
    is_one = lax.broadcasted_iota(jnp.int32, (LANE, images), 0) == width % LANE

    def exchange(zp, yp, k):
        to_pos = zp * RING + y if k == 0 else z * RING + yp
        b, a = (yp, z) if k == 0 else (zp, y)
        mine = (c == k) & (to_pos == pos)
        src = send.at[zp, 2 * yp + k]
        dst = recv.at[b, :, pl.ds(pl.multiple_of(a * 2 * LANE + c * LANE, LANE), LANE)]

        @pl.when(mine)
        def _():
            pltpu.make_async_copy(src, dst, recv_sem.at[b, a * 2 + c]).start()

        @pl.when(jnp.logical_not(mine))
        def _():
            pltpu.make_async_remote_copy(
                src_ref=src, dst_ref=dst,
                send_sem=send_sem.at[zp, 2 * yp + k], recv_sem=recv_sem.at[b, a * 2 + c],
                device_id={"img": 2 * x + k, "pos": to_pos}, device_id_type=MESH,
            ).start()

    def rows_of(q):
        return pl.ds(pl.multiple_of(q * piece, 8), piece)

    def x_copy(b, d):
        q = (x + d) % RING
        return pltpu.make_async_remote_copy(
            src_ref=part.at[b, rows_of(q)], dst_ref=x_recv.at[b, x],
            send_sem=x_send.at[b, q], recv_sem=x_sem.at[b, x],
            device_id={"img": 2 * q + c, "pos": pos}, device_id_type=MESH,
        )

    def b_copy(b):
        to_pos = (1 - c) * (z * RING + b) + c * (b * RING + y)
        return pltpu.make_async_remote_copy(
            src_ref=owned_sum.at[b], dst_ref=b_recv.at[ring_b],
            send_sem=b_send.at[b], recv_sem=b_sem.at[ring_b],
            device_id={"img": img, "pos": to_pos}, device_id_type=MESH,
        )

    row = lax.broadcasted_iota(jnp.int32, (LANE, LANE), 0)
    col = lax.broadcasted_iota(jnp.int32, (LANE, LANE), 1)

    def arrive(t):
        b = (ring_b + turn(t)) % RING
        for s in range(2 * RING):
            pltpu.make_async_copy(
                send.at[0, 0], recv.at[b, :, s * LANE:(s + 1) * LANE], recv_sem.at[b, s]
            ).wait()

    def gram(t):
        b = (ring_b + turn(t)) % RING
        for i in range(full + 1):
            height, wide = (LANE, (i + 1) * LANE) if i < full else (strip, full * LANE + strip)
            prod = lax.dot_general(
                recv[b, i * LANE:i * LANE + height, :], recv[b, :wide, :],
                (((1,), (1,)), ((), ())), preferred_element_type=F32,
            )
            for j in range(i + 1):
                first = place(i, j, full, strip)
                w = min(LANE, wide - j * LANE)
                block = prod[:, j * LANE:j * LANE + w]
                if i == j and i % 2 == 1:
                    at = place(full, full, full, strip) + strip + i // 2
                    part[b, at:at + 1, :] = jnp.sum(jnp.where(row == col, block, 0.0), axis=0, keepdims=True)
                    block = jnp.where(row >= col, part[b, first:first + LANE, :], block)
                part[b, first:first + height, :w] = block
        for d in (2, 1, 3):
            x_copy(b, d).start()

    def settle(t):
        b = (ring_b + turn(t)) % RING
        total = part[b, rows_of(x)]
        for d in (1, 3, 2):
            q = (x + d) % RING
            pltpu.make_async_copy(owned_sum.at[0], x_recv.at[b, q], x_sem.at[b, q]).wait()
            total = total + x_recv[b, q]
        owned_sum[b] = total

    def pick(t):
        zp = slab_of(t)
        load(t).wait()
        group = images

        def multiply(g, carry):
            at = pl.ds(pl.multiple_of(g * group, group), group)
            chunk = slab[t, at].reshape(group * owned, c_in)
            to = pl.ds(pl.multiple_of(g * group * owned, group * owned), group * owned)
            found = jnp.dot(chunk, onehot[...], preferred_element_type=F32)
            for l in range(cols // LANE):
                picked[l, to, :] = found[:, l * LANE:(l + 1) * LANE]
            return carry

        lax.fori_loop(0, images // group, multiply, 0)
        for j in range(owned):
            for l in range(cols // LANE):
                height = min(LANE, rows - l * LANE)
                block = picked[l, pl.ds(j, images, stride=owned), :].T[:height]
                if l == width // LANE:
                    block = jnp.where(is_one[:height], 1.0, block)
                block = jnp.where(usable[:height], block, 0.0)
                send[zp, j, l * LANE:l * LANE + height, :] = block.astype(BF16)

    def offer(t):
        zp = slab_of(t)
        for d in (1, 3):
            exchange(zp, (y + d) % RING, 0)

        @pl.when(t < 2)
        def _():
            for d in (1, 3, 2, 0):
                exchange(zp, (y + d) % RING, 1)

    def next_slab(t, carry):
        pick(t)
        offer(t)
        return carry

    pick(0)
    pl.semaphore_wait(barrier, 5 * (RING - 1) + 1)
    offer(0)
    lax.fori_loop(1, RING, next_slab, 0)

    def later(n):
        def one(i, carry):
            d = turn(i)
            exchange((z + d) % RING, (y + turn(n)) % RING, 0)
            exchange(slab_of(n), (y + d) % RING, 1)
            return carry

        lax.fori_loop(0, RING, one, 0)

    arrive(0)
    later(2)
    gram(0)

    def stage(t, carry):
        arrive(t)

        @pl.when(t == 1)
        def _():
            later(3)

        gram(t)
        settle(t - 1)
        b_copy((ring_b + turn(t - 1)) % RING).start()
        return carry

    lax.fori_loop(1, RING, stage, 0)
    settle(RING - 1)

    def ag_copy(d):
        q = (x + d) % RING
        return pltpu.make_async_remote_copy(
            src_ref=tot.at[c, rows_of(x)], dst_ref=tot.at[c, rows_of(x)],
            send_sem=ag_send.at[q], recv_sem=ag_sem.at[x],
            device_id={"img": 2 * q + c, "pos": pos}, device_id_type=MESH,
        )

    def fw_copy(q):
        return pltpu.make_async_remote_copy(
            src_ref=tot.at[c, rows_of(q)], dst_ref=tot.at[c, rows_of(q)],
            send_sem=fw_send.at[q], recv_sem=fw_sem.at[q],
            device_id={"img": 2 * x + 1 - c, "pos": pos}, device_id_type=MESH,
        )

    total = owned_sum[ring_b]
    for d in (1, 2, 3):
        b = (ring_b + d) % RING
        pltpu.make_async_copy(owned_sum.at[0], b_recv.at[b], b_sem.at[b]).wait()
        total = total + b_recv[b]
    tot[c, rows_of(x)] = total
    for d in (2, 1, 3):
        ag_copy(d).start()
    fw_copy(x).start()
    for d in (1, 3, 2):
        q = (x + d) % RING
        pltpu.make_async_copy(owned_sum.at[0], tot.at[c, rows_of(q)], ag_sem.at[q]).wait()
        fw_copy(q).start()
    for q in range(RING):
        pltpu.make_async_copy(owned_sum.at[0], tot.at[1 - c, rows_of(q)], fw_sem.at[q]).wait()

    def sent(t, carry):
        zp = slab_of(t)
        for j in range(owned):
            yp, k = j // 2, j % 2
            mine = (c == k) & ((zp == z) if k == 0 else (yp == y))

            @pl.when(jnp.logical_not(mine))
            def _():
                pltpu.make_async_copy(send.at[zp, j], send.at[zp, j], send_sem.at[zp, j]).wait()

        return carry

    lax.fori_loop(0, RING, sent, 0)
    for d in range(1, RING):
        b_copy((ring_b + d) % RING).wait_send()
        for b in range(RING):
            x_copy(b, d).wait_send()
        ag_copy(d).wait_send()
    for q in range(RING):
        fw_copy(q).wait_send()


def finish_kernel(width, tot, centres, covars, made, sem):
    rows, full, strip, packed = sizes(width)
    row = lax.broadcasted_iota(jnp.int32, (LANE, LANE), 0)
    col = lax.broadcasted_iota(jnp.int32, (LANE, LANE), 1)
    diagonals = place(full, full, full, strip) + strip

    def block(p, i, j):
        first = place(i, j, full, strip)
        if i == full:
            return tot[p, first:first + strip, :]
        both = tot[p, first:first + LANE, :]
        if i > j:
            return both
        if i % 2 == 0:
            return jnp.where(row >= col, both, both.T)
        at = diagonals + i // 2
        return jnp.where(row == col, tot[p, at:at + 1, :], jnp.where(row < col, both, both.T))

    mark = width - full * LANE
    copies, means = [], []
    for p in range(tot.shape[0]):
        lin = jnp.concatenate([block(p, full, j)[mark:mark + 1] for j in range(full + 1)], axis=1)
        n = block(p, full, full)[mark:mark + 1, mark:mark + 1]
        means.append((n, lin / n, 1.0 / (n - 1.0)))
        centres[p:p + 1, :] = means[p][1][:, :width]
    for i in range(full + 1):
        height = LANE if i < full else strip
        keep = min(height, width - i * LANE)
        for p in range(tot.shape[0]):
            n, centre, scale = means[p]
            parts = [block(p, i, j) for j in range(i + 1)]
            for j in range(i + 1, full + 1):
                flip = block(p, j, i).T
                if flip.shape[1] < LANE:
                    flip = jnp.concatenate([flip, jnp.zeros((height, LANE - flip.shape[1]), F32)], axis=1)
                parts.append(flip)
            sums = jnp.concatenate(parts, axis=1)
            own = sums[:, width:width + 1] / n
            spread = (sums - (n * own) * centre) * scale
            at = lax.broadcasted_iota(jnp.int32, sums.shape, 0) + i * LANE
            across = lax.broadcasted_iota(jnp.int32, sums.shape, 1)
            spread = spread + jnp.where(at == across, REG, 0.0)
            made[i * LANE:i * LANE + height, p, :] = spread[:, :width]
        rows_made = slice(i * LANE, i * LANE + keep)
        copies.append(pltpu.make_async_copy(made.at[rows_made], covars.at[rows_made], sem.at[i]))
        copies[-1].start()
    for copy in copies:
        copy.wait()


def body(features, channel_index, image_counts):
    images, positions, c_in = features.shape
    width = channel_index.shape[0]
    rows, full, strip, packed = sizes(width)
    cols = -(-rows // LANE) * LANE
    owned = positions // RING
    dma = pltpu.SemaphoreType.DMA
    tot = pl.pallas_call(
        functools.partial(gather_kernel, width),
        out_shape=pltpu.VMEM((2, packed, LANE), F32),
        in_specs=[
            pl.BlockSpec(memory_space=pl.ANY),
            pl.BlockSpec(memory_space=pltpu.VMEM),
            pl.BlockSpec(memory_space=pltpu.SMEM),
        ],
        out_specs=pl.BlockSpec(memory_space=pltpu.VMEM),
        scratch_shapes=[
            pltpu.VMEM((RING, images, owned, c_in), BF16),
            pltpu.VMEM((c_in, cols), BF16),
            pltpu.VMEM((cols // LANE, images * owned, LANE), F32),
            pltpu.VMEM((RING, owned, rows, images), BF16),
            pltpu.VMEM((RING, rows, 2 * RING * LANE), BF16),
            pltpu.VMEM((RING, packed, LANE), F32),
            pltpu.VMEM((RING, RING, packed // RING, LANE), F32),
            pltpu.VMEM((RING, packed // RING, LANE), F32),
            pltpu.VMEM((RING, packed // RING, LANE), F32),
            dma((RING,)),
            dma((RING, owned)),
            dma((RING, 2 * RING)),
            dma((RING, RING)), dma((RING, RING)),
            dma((RING,)), dma((RING,)),
            dma((RING,)), dma((RING,)),
            dma((RING,)), dma((RING,)),
        ],
        compiler_params=pltpu.CompilerParams(
            collective_id=0, has_side_effects=True, vmem_limit_bytes=56 * 2**20
        ),
        name="pick_and_sum",
    )(features, channel_index, image_counts)
    centres, covars = pl.pallas_call(
        functools.partial(finish_kernel, width),
        out_shape=(
            jax.ShapeDtypeStruct((2, width), F32),
            jax.ShapeDtypeStruct((width, 2, width), F32),
        ),
        in_specs=[pl.BlockSpec(memory_space=pltpu.VMEM)],
        out_specs=(pl.BlockSpec(memory_space=pltpu.VMEM), pl.BlockSpec(memory_space=pl.ANY)),
        scratch_shapes=[pltpu.VMEM((full * LANE + strip, 2, width), F32), dma((full + 1,))],
        compiler_params=pltpu.CompilerParams(vmem_limit_bytes=40 * 2**20),
        name="finish",
    )(tot)
    return centres, jnp.transpose(covars, (1, 0, 2))


def solution(mesh):
    placed = (P(("img", "pos"), None, None), P(), P(("img", "pos")))
    return jax.shard_map(
        body,
        mesh=mesh,
        in_specs=placed,
        out_specs=(P("pos", None), P("pos", None, None)),
        check_vma=False,
    )
```
